128 devices in a mesh: stream: 8 (over x, z_lo), span: 16 (over y, z_hi, core).
Axes of the slice: x: 4, y: 4, z: 4 (z_hi: 2, z_lo: 2; z = z_hi * 2 + z_lo), core: 2. Of those that a mesh axis runs over, the one named last changes fastest.
Arguments:
- right_side: float32 [4, 262144], P(None, ('stream', 'span')), may hold values from -5 to 6
- fine_values: float32 [8, 4, 4, 262144], P(None, None, None, ('stream', 'span')), as said below
- fine_columns: int32 [8, 262144], P(None, ('stream', 'span')), may hold values from 0 to 2303, as said below
- fine_sends: int32 [4, 8192], P(None, ('stream', 'span')), may hold values from 0 to 2047, as said below
- fine_order: int32 [128, 2048], P(('stream', 'span')), may hold values from 0 to 2047, each once within a row
- fine_weights: float32 [4, 4, 262144], P(None, None, ('stream', 'span')), may hold values from -0.6 to 1.2
- middle_values: float32 [8, 4, 4, 65536], P(None, None, None, ('stream', 'span')), as said below
- middle_columns: int32 [8, 65536], P(None, ('stream', 'span')), may hold values from 0 to 767, as said below
- middle_sends: int32 [4, 8192], P(None, ('stream', 'span')), may hold values from 0 to 511, as said below
- middle_order: int32 [128, 512], P(('stream', 'span')), may hold values from 0 to 511, each once within a row
- middle_weights: float32 [4, 4, 65536], P(None, None, ('stream', 'span')), may hold values from -0.6 to 1.2
- coarsest_values: float32 [8, 4, 4, 16384], P(None, None, None, ('stream', 'span')), as said below
- coarsest_columns: int32 [8, 16384], P(None, ('stream', 'span')), may hold values from 0 to 2047, as said below
Outputs:
- solution: float32 [4, 262144], P(None, ('stream', 'span'))
- residual: float32 [4, 262144], P(None, ('stream', 'span'))
The draws below stay inside these ranges and needn't reach their ends.
Inputs may be any that keep to these rules, and one draw needn't show every extreme that they name: `fine_sends`: entry [d, p * 64 + s] is a local row block of device p sent in direction d (0: lower stream index, 1: higher stream index, 2: lower span index, 3: higher span index). Each list has a length of at most 64, which differs between devices and directions and is 64 on some device; rows may repeat within a list, and the slots at or after the length repeat the list's slot 0 as padding. `middle_sends`: as for the first level, with local row blocks of the second level. `fine_columns`: block k = 0 of row block n names its own local row. Entries below 2048 are local row blocks; an entry 2048 + e * 64 + s names slot s of halo block e. Where halo block e has a sending device, s is below the length of that device's list; where it has none (the block is zero), s may be any slot below 64. `middle_columns`: as for the first level with 512 local row blocks. `coarsest_columns`: block k = 0 names the row block itself within its slab; the others name row blocks of the same slab. `fine_values`: each diagonal entry of the k = 0 block is 1 or more, and the other 31 entries of its row over all 8 blocks have absolute values summing to at most 0.9 times it. `middle_values`: as for the first level. `coarsest_values`: as for the first level.
All inputs are finite; a program needn't handle non-finite values.
Results may differ from the reference program's by a relative error of at most 0.0003.
Values sent between devices are 32-bit elements; how exact they have to be, the bound alone decides.
A program may use at most 64 MiB of HBM per device.

```python
import jax
import jax.numpy as jnp
from jax import lax

NNZ = 8
R1 = 2048
KSM = 3
KC = 4
R2 = 512
R3 = 128
H = 64
SLABS = 8
GROUP = 16
DEVS = 128
N1 = 262144
N2 = 65536
N3 = 16384


def halo_counts(key, salt_value):
    sub_key = jax.random.fold_in(key, 40 + salt_value)
    counts = jax.random.randint(sub_key, (DEVS, 4), H // 2, H + 1)
    chosen = jax.random.randint(jax.random.fold_in(sub_key, 1), (), 0, DEVS)
    return jnp.where(jnp.arange(DEVS)[:, None] == chosen, H, counts)


def received_counts(counts):
    device = jnp.arange(DEVS)
    slab_index = device // GROUP
    member = device % GROUP
    from_prev = (slab_index - 1) % SLABS * GROUP + member
    from_next = (slab_index + 1) % SLABS * GROUP + member
    span_prev = slab_index * GROUP + jnp.maximum(member - 1, 0)
    span_next = slab_index * GROUP + jnp.minimum(member + 1, GROUP - 1)
    return jnp.stack([counts[from_prev, 1], counts[from_next, 0], counts[span_prev, 3], counts[span_next, 2]], axis=1)


def send_lists(key, salt_value, row_count):
    counts = halo_counts(key, salt_value)
    raw_rows = jax.random.randint(jax.random.fold_in(key, 60 + salt_value), (DEVS, 4, H), 0, row_count)
    raw_rows = raw_rows.at[:, 0, 0].set(row_count - 1)
    raw_rows = raw_rows.at[:, 0, 1].set(0)
    slot_index = jnp.arange(H)[None, None, :]
    send_table = jnp.where(slot_index < counts[:, :, None], raw_rows, raw_rows[:, :, :1])
    return jnp.transpose(send_table, (1, 0, 2)).reshape(4, DEVS * H).astype(jnp.int32)


def column_lists(key, salt_value, row_count):
    received = received_counts(halo_counts(key, salt_value))
    draw_shape = (NNZ - 1, DEVS, row_count)
    base_key = jax.random.fold_in(key, 80 + salt_value)
    local_rows = jax.random.randint(jax.random.fold_in(base_key, 0), draw_shape, 0, row_count)
    remote_mask = jax.random.randint(jax.random.fold_in(base_key, 1), draw_shape, 0, 4) == 0
    direction = jax.random.randint(jax.random.fold_in(base_key, 2), draw_shape, 0, 4)
    slot_limit = received[jnp.arange(DEVS)[None, :, None], direction]
    slot_index = jax.random.randint(jax.random.fold_in(base_key, 3), draw_shape, 0, slot_limit)
    others = jnp.where(remote_mask, row_count + direction * H + slot_index, local_rows)
    own_rows = jnp.broadcast_to(jnp.arange(row_count)[None, None, :], (1, DEVS, row_count))
    columns = jnp.concatenate([own_rows, others], axis=0).reshape(NNZ, DEVS * row_count)
    columns = columns.at[NNZ - 1, DEVS * row_count - 1].set(row_count + 4 * H - 1)
    return columns.astype(jnp.int32)


def block_values(key, salt_value, total_rows):
    base_key = jax.random.fold_in(key, salt_value)
    row_scale = jnp.exp(jax.random.uniform(jax.random.fold_in(base_key, 0), (4, total_rows), minval=0.0, maxval=jnp.log(10.0)))
    spread = jax.random.uniform(jax.random.fold_in(base_key, 1), (NNZ, 4, 4, total_rows), minval=0.1, maxval=1.0)
    share = jax.random.uniform(jax.random.fold_in(base_key, 2), (4, total_rows), minval=0.86, maxval=0.89)
    block_index = jnp.arange(NNZ)[:, None, None, None]
    row_index = jnp.arange(4)[None, :, None, None]
    col_index = jnp.arange(4)[None, None, :, None]
    on_diagonal = (block_index == 0) & (row_index == col_index)
    spread = jnp.where(on_diagonal, 0.0, spread)
    row_total = jnp.sum(spread, axis=(0, 2))
    scaled = row_scale[None, :, None, :]
    off_part = -(share / row_total)[None, :, None, :] * spread * scaled
    return jnp.where(on_diagonal, scaled, off_part).astype(jnp.float32)


def prolong_weights(key, salt_value, total_rows):
    base_key = jax.random.fold_in(key, 20 + salt_value)
    on_diagonal = (jnp.arange(4)[:, None] == jnp.arange(4)[None, :])[:, :, None]
    rough_part = jnp.clip(0.2 * jax.random.normal(base_key, (4, 4, total_rows)), -0.6, 0.6)
    return (jnp.where(on_diagonal, 0.6, 0.0) + rough_part).astype(jnp.float32)


def draw_right_side(key, part):
    base_key = jax.random.fold_in(key, 7)
    rough_part = jnp.clip(jax.random.normal(base_key, (4, N1)), -5.5, 5.5)
    return (0.5 + rough_part).astype(jnp.float32)


def draw_fine_weights(key, part):
    return prolong_weights(key, 1, N1)


def draw_middle_weights(key, part):
    return prolong_weights(key, 2, N2)


def draw_fine_values(key, part):
    return block_values(key, 1, N1)


def draw_middle_values(key, part):
    return block_values(key, 2, N2)


def draw_coarsest_values(key, part):
    return block_values(key, 3, N3)


def draw_fine_columns(key, part):
    return column_lists(key, 1, R1)


def draw_middle_columns(key, part):
    return column_lists(key, 2, R2)


def draw_fine_sends(key, part):
    return send_lists(key, 1, R1)


def draw_middle_sends(key, part):
    return send_lists(key, 2, R2)


def draw_coarsest_columns(key, part):
    base_key = jax.random.fold_in(key, 95)
    group_rows = GROUP * R3
    own_rows = jnp.arange(N3) % group_rows
    others = jax.random.randint(base_key, (NNZ - 1, N3), 0, group_rows)
    columns = jnp.concatenate([own_rows[None, :], others], axis=0)
    columns = columns.at[NNZ - 1, 0].set(group_rows - 1)
    return columns.astype(jnp.int32)


def setup_inputs(seed: int = 0) -> dict:
    key_of = jax.random.split(jax.random.key(seed), 14)
    right_side = draw_right_side(jax.random.fold_in(key_of[13], 71), 0)
    fine_values = draw_fine_values(jax.random.fold_in(key_of[13], 71), 0)
    fine_columns = draw_fine_columns(jax.random.fold_in(key_of[13], 71), 0)
    fine_sends = draw_fine_sends(jax.random.fold_in(key_of[13], 71), 0)
    fine_order = jax.vmap(lambda own: jax.random.permutation(own, R1))(jax.random.split(key_of[4], DEVS)).reshape((DEVS, R1)).astype(jnp.int32)
    fine_weights = draw_fine_weights(jax.random.fold_in(key_of[13], 71), 0)
    middle_values = draw_middle_values(jax.random.fold_in(key_of[13], 71), 0)
    middle_columns = draw_middle_columns(jax.random.fold_in(key_of[13], 71), 0)
    middle_sends = draw_middle_sends(jax.random.fold_in(key_of[13], 71), 0)
    middle_order = jax.vmap(lambda own: jax.random.permutation(own, R2))(jax.random.split(key_of[9], DEVS)).reshape((DEVS, R2)).astype(jnp.int32)
    middle_weights = draw_middle_weights(jax.random.fold_in(key_of[13], 71), 0)
    coarsest_values = draw_coarsest_values(jax.random.fold_in(key_of[13], 71), 0)
    coarsest_columns = draw_coarsest_columns(jax.random.fold_in(key_of[13], 71), 0)
    return {"right_side": right_side, "fine_values": fine_values, "fine_columns": fine_columns, "fine_sends": fine_sends, "fine_order": fine_order, "fine_weights": fine_weights, "middle_values": middle_values, "middle_columns": middle_columns, "middle_sends": middle_sends, "middle_order": middle_order, "middle_weights": middle_weights, "coarsest_values": coarsest_values, "coarsest_columns": coarsest_columns}


CHEB_CENTRE = 1.0
CHEB_RADIUS = 0.9


def chebyshev(operate, inverse_diag, target, initial, degree):
    sigma_value = CHEB_CENTRE / CHEB_RADIUS
    rho_prev = 1.0 / sigma_value
    if initial is None:
        iterate = jnp.zeros_like(target)
        current = target
    else:
        iterate = initial
        current = target - operate(initial)
    update = inverse_diag * current / CHEB_CENTRE
    iterate = iterate + update
    for _ in range(degree - 1):
        rho_next = 1.0 / (2.0 * sigma_value - rho_prev)
        current = target - operate(iterate)
        update = (rho_next * rho_prev) * update + (2.0 * rho_next / CHEB_RADIUS) * (inverse_diag * current)
        iterate = iterate + update
        rho_prev = rho_next
    return iterate


def inverse_diagonal(values):
    identity = jnp.eye(4, dtype=values.dtype)
    return 1.0 / jnp.sum(values[0] * identity[:, :, None], axis=1)


def global_columns(columns, row_count):
    position = jnp.arange(columns.shape[1], dtype=jnp.int32)
    device = (position // row_count)[None, :]
    inside = device * row_count + columns
    outside = DEVS * row_count + device * (4 * H) + (columns - row_count)
    return jnp.where(columns < row_count, inside, outside).astype(jnp.int32)


def halo_blocks(vector, send_rows, row_count):
    position = jnp.arange(DEVS * H, dtype=jnp.int32)
    sources = ((position // H)[None, :] * row_count + send_rows).astype(jnp.int32)
    outgoing = vector[:, sources].reshape(4, 4, SLABS, GROUP, H)
    from_prev = jnp.roll(outgoing[:, 1], 1, axis=1)
    from_next = jnp.roll(outgoing[:, 0], -1, axis=1)
    zero_row = jnp.zeros_like(outgoing[:, 2, :, :1])
    span_prev = jnp.concatenate([zero_row, outgoing[:, 3, :, :-1]], axis=2)
    span_next = jnp.concatenate([outgoing[:, 2, :, 1:], zero_row], axis=2)
    stacked = jnp.stack([from_prev, from_next, span_prev, span_next], axis=3)
    return stacked.reshape(4, DEVS * 4 * H)


def apply_level(vector, values, wide_cols, send_rows, row_count):
    extended_vec = jnp.concatenate([vector, halo_blocks(vector, send_rows, row_count)], axis=1)
    gathered = extended_vec[:, wide_cols]
    return jnp.einsum("kijn,jkn->in", values, gathered, precision=lax.Precision.HIGHEST)


def global_order(order_rows, row_count):
    return (jnp.arange(DEVS, dtype=jnp.int32)[:, None] * row_count + order_rows).reshape(-1).astype(jnp.int32)


def restrict(fine_vec, weights, positions):
    moved = fine_vec[:, positions]
    moved_weights = weights[:, :, positions]
    summed = jnp.einsum("ijn,in->jn", moved_weights, moved, precision=lax.Precision.HIGHEST)
    return summed.reshape(4, -1, 4).sum(axis=2)


def prolong(coarse, weights, positions):
    spread = jnp.repeat(coarse, 4, axis=1)
    moved_weights = weights[:, :, positions]
    placed = jnp.einsum("ijn,jn->in", moved_weights, spread, precision=lax.Precision.HIGHEST)
    return jnp.zeros_like(placed).at[:, positions].set(placed)


def reference(right_side, fine_values, fine_columns, fine_sends, fine_order, fine_weights, middle_values, middle_columns, middle_sends, middle_order, middle_weights, coarsest_values, coarsest_columns):
    fine_wide = global_columns(fine_columns, R1)
    middle_wide = global_columns(middle_columns, R2)
    group_rows = GROUP * R3
    slab_of = (jnp.arange(N3, dtype=jnp.int32) // group_rows)[None, :]
    coarse_wide = (slab_of * group_rows + coarsest_columns).astype(jnp.int32)

    def fine_apply(vector):
        return apply_level(vector, fine_values, fine_wide, fine_sends, R1)

    def middle_apply(vector):
        return apply_level(vector, middle_values, middle_wide, middle_sends, R2)

    def coarse_apply(vector):
        return jnp.einsum("kijn,jkn->in", coarsest_values, vector[:, coarse_wide], precision=lax.Precision.HIGHEST)

    fine_inv = inverse_diagonal(fine_values)
    middle_inv = inverse_diagonal(middle_values)
    coarse_inv = inverse_diagonal(coarsest_values)
    fine_pos = global_order(fine_order, R1)
    middle_pos = global_order(middle_order, R2)

    first_iter = chebyshev(fine_apply, fine_inv, right_side, None, KSM)
    fine_resid = right_side - fine_apply(first_iter)
    middle_rhs = restrict(fine_resid, fine_weights, fine_pos)
    middle_iter = chebyshev(middle_apply, middle_inv, middle_rhs, None, KSM)
    middle_resid = middle_rhs - middle_apply(middle_iter)
    coarse_rhs = restrict(middle_resid, middle_weights, middle_pos)
    coarse_iter = chebyshev(coarse_apply, coarse_inv, coarse_rhs, None, KC)
    middle_start = middle_iter + prolong(coarse_iter, middle_weights, middle_pos)
    middle_final = chebyshev(middle_apply, middle_inv, middle_rhs, middle_start, KSM)
    fine_start = first_iter + prolong(middle_final, fine_weights, fine_pos)
    solution = chebyshev(fine_apply, fine_inv, right_side, fine_start, KSM)
    residual = right_side - fine_apply(solution)
    return solution, residual
```

```python
import functools

import jax
import jax.numpy as jnp
from jax import lax
from jax.experimental import pallas as pl
from jax.experimental.pallas import tpu as pltpu
from jax.sharding import PartitionSpec as P

KSM = 3
KC = 4
CHEB_CENTRE = 1.0
CHEB_RADIUS = 0.9
LANES = 128
HALF = 64
MESH = pl.DeviceIdType.MESH


def chebyshev_factors(degree):
    sigma_value = CHEB_CENTRE / CHEB_RADIUS
    rho_prev = 1.0 / sigma_value
    factors = []
    for _ in range(degree - 1):
        rho_next = 1.0 / (2.0 * sigma_value - rho_prev)
        factors.append((rho_next * rho_prev, 2.0 * rho_next / CHEB_RADIUS))
        rho_prev = rho_next
    return factors


def gather_lanes(table, places):
    return jnp.take_along_axis(table, places, axis=1, mode="promise_in_bounds")


def row_of(ref, row):
    return jnp.broadcast_to(ref[pl.ds(row, 1), :], (8, LANES))


def lookup(tables, low, high, base=0, start=None):
    picked = start
    for h, table in enumerate(tables):
        taken = gather_lanes(table, low)
        picked = taken if picked is None else jnp.where(high == h + base, taken, picked)
    return picked


def cycle_kernel(
    tiles1, tiles2, streams, spans,
    right_hbm, values1_hbm, columns1_hbm, sends1_hbm, order1_hbm, weights1_hbm,
    values2_hbm, columns2_hbm, sends2_hbm, order2_hbm, weights2_hbm,
    values3_hbm, columns3_hbm,
    solution_ref, residual_ref,
    right_in, values1_in, columns1_in, sends1_in, order1_in, weights1_in,
    values2_in, columns2_in, sends2_in, order2_in, weights2_in,
    values3_in, columns3_in,
    right1, values1, columns1, picks1, restrict1, prolong1, weights1, inv1,
    values2, columns2, picks2, restrict2, prolong2, weights2, inv2,
    order_rows, table1, table2, first1, first2, right2, part1, part2, product1, product2,
    outgoing, incoming, halo, gathered, group_own, group_all, table3, inv3,
    in_sem, send_sem, recv_sem, group_send_sem, group_recv_sem,
):
    a = lax.axis_index("stream")
    b = lax.axis_index("span")
    prev_a, next_a = lax.rem(a + streams - 1, streams), lax.rem(a + 1, streams)
    prev_b, next_b = lax.rem(b + spans - 1, spans), lax.rem(b + 1, spans)

    barrier = pltpu.get_barrier_semaphore()
    for who in (prev_a, next_a):
        pl.semaphore_signal(barrier, inc=1, device_id=(who, b), device_id_type=MESH)
    for step in range(1, spans):
        pl.semaphore_signal(
            barrier, inc=1, device_id=(a, lax.rem(b + step, spans)), device_id_type=MESH
        )

    loads = [
        pltpu.make_async_copy(src, dst, in_sem.at[n])
        for n, (src, dst) in enumerate(
            (
                (right_hbm, right_in), (values1_hbm, values1_in), (columns1_hbm, columns1_in),
                (sends1_hbm, sends1_in), (order1_hbm, order1_in), (weights1_hbm, weights1_in),
                (values2_hbm, values2_in), (columns2_hbm, columns2_in), (sends2_hbm, sends2_in),
                (order2_hbm, order2_in), (weights2_hbm, weights2_in),
                (values3_hbm, values3_in), (columns3_hbm, columns3_in),
            )
        )
    ]
    for load in loads:
        load.start()
    for load in loads:
        load.wait()

    lane = lax.broadcasted_iota(jnp.int32, (8, LANES), 1)
    row = lax.broadcasted_iota(jnp.int32, (8, LANES), 0)

    def dense_blocks(source, target, tiles):
        for k in range(8):
            for i in range(4):
                for t in range(tiles):
                    target[pl.ds((k * 16 + i * 4) * tiles + t, 4, stride=tiles), :] = source[
                        k, i, :, t * LANES : (t + 1) * LANES
                    ]

    def dense_weights(source, target, tiles):
        for i in range(4):
            for t in range(tiles):
                target[pl.ds(i * 4 * tiles + t, 4, stride=tiles), :] = source[
                    i, :, t * LANES : (t + 1) * LANES
                ]

    dense_blocks(values1_in, values1, tiles1)
    for t in range(tiles1):
        right1[pl.ds(t, 4, stride=tiles1), :] = right_in[:, t * LANES : (t + 1) * LANES]
        columns1[pl.ds(t, 8, stride=tiles1), :] = columns1_in[:, t * LANES : (t + 1) * LANES]
    for i in range(4):
        inv1[pl.ds(i * tiles1, tiles1), :] = 1.0 / values1[pl.ds(i * 5 * tiles1, tiles1), :]

    def pick_places(sends):
        stream_part = jnp.concatenate([sends[1:2, :], sends[0:1, :]], axis=1)
        span_part = jnp.concatenate([sends[3:4, :], sends[2:3, :]], axis=1)
        return jnp.where(
            row < 4,
            jnp.broadcast_to(stream_part, (8, LANES)),
            jnp.broadcast_to(span_part, (8, LANES)),
        )

    picks1[...] = pick_places(sends1_in)
    picks2[...] = pick_places(sends2_in)

    for i in range(4):
        for k in range(8):
            for t in range(tiles2):
                values2[pl.ds(i * 32 * tiles2 + k * tiles2 + t, 4, stride=8 * tiles2), :] = (
                    values2_in[k, i, :, t * LANES : (t + 1) * LANES]
                )
    for t in range(tiles2):
        columns2[pl.ds(t, 8, stride=tiles2), :] = columns2_in[:, t * LANES : (t + 1) * LANES]
    for i in range(4):
        inv2[pl.ds(i * tiles2, tiles2), :] = 1.0 / values2[pl.ds(i * 5 * 8 * tiles2, tiles2), :]
    dense_weights(weights1_in, weights1, tiles1)
    dense_weights(weights2_in, weights2, tiles2)

    quad = lane // 32
    for t in range(tiles1):
        order_rows[pl.ds(t, 1), :] = order1_in[:, t * LANES : (t + 1) * LANES]
    for pair in range(2):
        entry = row // 4 + 2 * pair
        low = (lane * 4 + entry) % LANES
        found = None
        for q in range(4):
            rows = order_rows[pl.ds(q, 4, stride=4), :]
            taken = gather_lanes(jnp.concatenate([rows, rows], axis=0), low)
            found = taken if found is None else jnp.where(quad == q, taken, found)
        restrict1[pl.ds(pair * 8, 8), :] = found

    def inverse_order(rows_ref, count, tiles):
        total = jnp.zeros((2 * tiles, LANES), jnp.float32)
        for t in range(count):
            own = rows_ref[pl.ds(t, 1), :]
            tile_ids = lax.broadcasted_iota(jnp.int32, (tiles, LANES), 0)
            member = (jnp.broadcast_to(own // LANES, (tiles, LANES)) == tile_ids)
            lanes = lax.broadcasted_iota(jnp.int32, (tiles, LANES), 1)
            small = jnp.where(member, (lanes // 4).astype(jnp.float32), 0.0)
            large = jnp.where(member, float(t), 0.0)
            left = jnp.concatenate([small, large], axis=0)
            low_ids = lax.broadcasted_iota(jnp.int32, (LANES, LANES), 0)
            right = jnp.where(
                jnp.broadcast_to(own % LANES, (LANES, LANES)) == low_ids, 1.0, 0.0
            )
            total = total + lax.dot_general(
                left.astype(jnp.bfloat16),
                right.astype(jnp.bfloat16),
                (((1,), (1,)), ((), ())),
                preferred_element_type=jnp.float32,
            )
        return (total[:tiles] + 32.0 * total[tiles:]).astype(jnp.int32)

    prolong1[...] = inverse_order(order_rows, tiles1, tiles1)

    for t in range(tiles2):
        order_rows[pl.ds(t, 1), :] = order2_in[:, t * LANES : (t + 1) * LANES]
    low = (lane * 4 + row % 4) % LANES
    found = None
    for q in range(4):
        taken = gather_lanes(row_of(order_rows, q), low)
        found = taken if found is None else jnp.where(quad == q, taken, found)
    restrict2[...] = found
    prolong2[...] = inverse_order(order_rows, tiles2, 8)

    pl.semaphore_wait(barrier, spans + 1)

    sends = []

    def copies_of(x):
        places = (
            (1, (prev_a, b)),
            (0, (next_a, b)),
            (3, (a, prev_b)),
            (2, (a, next_b)),
        )
        return [
            pltpu.make_async_remote_copy(
                src_ref=outgoing.at[x],
                dst_ref=incoming.at[x, slot],
                send_sem=send_sem.at[x, slot],
                recv_sem=recv_sem.at[x, slot],
                device_id=who,
                device_id_type=MESH,
            )
            for slot, who in places
        ]

    def exchange_start(x, table, picks, tiles):
        places = picks[...]
        tables = [table[pl.ds(h, 8, stride=tiles), :] for h in range(tiles)]
        outgoing[x] = lookup(tables, places % LANES, places // LANES)
        for copy in copies_of(x):
            copy.start()
            sends.append(copy)

    def exchange_end(x):
        for copy in copies_of(x):
            copy.wait_recv()
        first_half = lane < HALF
        block2 = jnp.where(b > 0, incoming[x, 2], 0.0)
        block3 = jnp.where(b < spans - 1, incoming[x, 3], 0.0)
        halo[...] = jnp.where(
            row < 4,
            jnp.where(first_half, incoming[x, 0], incoming[x, 1]),
            jnp.where(first_half, block2, block3),
        )

    def store_table(table, vector, tiles):
        table[pl.ds(0, 4 * tiles), :] = vector
        table[pl.ds(4 * tiles, 4 * tiles), :] = vector

    def operate1(x):
        exchange_start(x, table1, picks1, tiles1)

        def local(group, carry):
            where_to = columns1[pl.ds(pl.multiple_of(group * 8, 8), 8), :]
            low, high = where_to % LANES, where_to // LANES
            for j in range(4):
                gathered[j, pl.ds(pl.multiple_of(group * 8, 8), 8), :] = lookup(
                    [row_of(table1, j * tiles1 + h) for h in range(tiles1)], low, high
                )
            return carry

        lax.fori_loop(0, tiles1, local, 0)
        exchange_end(x)

        def remote(part, carry):
            sums = [None] * 4
            for k in range(8):
                start = k * tiles1 + part * 8
                here = pl.ds(pl.multiple_of(start, 8), 8)
                where_to = columns1[here, :]
                low, high = where_to % LANES, where_to // LANES
                for j in range(4):
                    found = lookup(
                        [row_of(halo, j), row_of(halo, 4 + j)],
                        low, high, tiles1, gathered[j, here, :],
                    )
                    for i in range(4):
                        at = (k * 16 + i * 4 + j) * tiles1 + part * 8
                        term = values1[pl.ds(pl.multiple_of(at, 8), 8), :] * found
                        sums[i] = term if sums[i] is None else sums[i] + term
            for i in range(4):
                part1[pl.ds(pl.multiple_of(i * tiles1 + part * 8, 8), 8), :] = sums[i]
            return carry

        lax.fori_loop(0, tiles1 // 8, remote, 0)
        return part1[...]

    def operate2(x):
        exchange_start(x, table2, picks2, tiles2)
        groups = 8 * tiles2 // 8

        def local(group, carry):
            where_to = columns2[pl.ds(pl.multiple_of(group * 8, 8), 8), :]
            low, high = where_to % LANES, where_to // LANES
            for j in range(4):
                gathered[j, pl.ds(pl.multiple_of(group * 8, 8), 8), :] = lookup(
                    [row_of(table2, j * tiles2 + h) for h in range(tiles2)], low, high
                )
            return carry

        lax.fori_loop(0, groups, local, 0)
        exchange_end(x)
        sums = [None] * 4
        for group in range(groups):
            here = pl.ds(group * 8, 8)
            where_to = columns2[here, :]
            low, high = where_to % LANES, where_to // LANES
            for j in range(4):
                found = lookup(
                    [row_of(halo, j), row_of(halo, 4 + j)],
                    low, high, tiles2, gathered[j, here, :],
                )
                for i in range(4):
                    term = values2[pl.ds((i * 4 + j) * 8 * tiles2 + group * 8, 8), :] * found
                    sums[i] = term if sums[i] is None else sums[i] + term
        for i in range(4):
            part2[pl.ds(i * tiles2, tiles2), :] = sums[i][:4] + sums[i][4:]
        return part2[...]

    def smooth(operate, table, tiles, right, inv, first, x):
        if first:
            update = inv[...] * right[...]
            store_table(table, update, tiles)
        else:
            update = inv[...] * (right[...] - operate(x))
            x += 1
            store_table(table, table[pl.ds(0, 4 * tiles), :] + update, tiles)
        for keep, gain in chebyshev_factors(KSM):
            current = right[...] - operate(x)
            x += 1
            update = keep * update + gain * (inv[...] * current)
            store_table(table, table[pl.ds(0, 4 * tiles), :] + update, tiles)
        return x

    x = smooth(operate1, table1, tiles1, right1, inv1, True, 0)
    first1[...] = table1[pl.ds(0, 4 * tiles1), :]
    resid = right1[...] - operate1(x)
    x += 1
    part1[...] = resid
    for j in range(4):
        total = None
        for i in range(4):
            term = (
                weights1[pl.ds((i * 4 + j) * tiles1, tiles1), :]
                * part1[pl.ds(i * tiles1, tiles1), :]
            )
            total = term if total is None else total + term
        product1[pl.ds(j * tiles1, tiles1), :] = total
    for j in range(4):
        tables = [row_of(product1, j * tiles1 + h) for h in range(tiles1)]
        total = None
        for pair in range(2):
            where_to = restrict1[pl.ds(pair * 8, 8), :]
            taken = lookup(tables, where_to % LANES, where_to // LANES)
            total = taken if total is None else total + taken
        right2[pl.ds(j * tiles2, tiles2), :] = total[:4] + total[4:]

    x = smooth(operate2, table2, tiles2, right2, inv2, True, x)
    first2[...] = table2[pl.ds(0, 4 * tiles2), :]
    resid = right2[...] - operate2(x)
    x += 1
    part2[...] = resid
    for j in range(4):
        total = None
        for i in range(4):
            term = (
                weights2[pl.ds((i * 4 + j) * tiles2, tiles2), :]
                * part2[pl.ds(i * tiles2, tiles2), :]
            )
            total = term if total is None else total + term
        product2[pl.ds(j * tiles2, tiles2), :] = total
    where_to = restrict2[...]
    for j in range(4):
        tables = [row_of(product2, j * tiles2 + h) for h in range(tiles2)]
        taken = lookup(tables, where_to % LANES, where_to // LANES)
        table3[pl.ds(j, 1), :] = jnp.sum(taken[:4], axis=0, keepdims=True)

    right3 = table3[...]
    for i in range(4):
        inv3[pl.ds(i, 1), :] = 1.0 / values3_in[0, i, i : i + 1, :]
    update = inv3[...] * right3
    vector = update
    columns3 = columns3_in[...]
    low3, high3 = columns3 % LANES, columns3 // LANES
    for turn, (keep, gain) in enumerate(chebyshev_factors(KC)):
        group_own[turn] = vector
        copies = []
        for step in range(1, spans):
            copies.append(
                pltpu.make_async_remote_copy(
                    src_ref=group_own.at[turn],
                    dst_ref=group_all.at[turn, step],
                    send_sem=group_send_sem.at[turn, step],
                    recv_sem=group_recv_sem.at[turn, step],
                    device_id=(a, lax.rem(b + step, spans)),
                    device_id_type=MESH,
                )
            )
        for copy in copies:
            copy.start()
            sends.append(copy)
        for copy in copies:
            copy.wait_recv()
        distance = lax.rem(b - high3 + spans, spans)
        picked = []
        for j in range(4):
            tables = [row_of(group_own.at[turn], j)] + [
                row_of(group_all.at[turn, step], j) for step in range(1, spans)
            ]
            picked.append(lookup(tables, low3, distance))
        for i in range(4):
            total = None
            for j in range(4):
                term = values3_in[:, i, j, :] * picked[j]
                total = term if total is None else total + term
            table3[pl.ds(i, 1), :] = jnp.sum(total, axis=0, keepdims=True)
        current = right3 - table3[...]
        update = keep * update + gain * (inv3[...] * current)
        vector = vector + update

    table3[...] = vector
    back = prolong2[...]
    spread = [gather_lanes(row_of(table3, j), back) for j in range(4)]
    for i in range(4):
        total = first2[pl.ds(i * tiles2, tiles2), :]
        for j in range(4):
            total = total + weights2[pl.ds((i * 4 + j) * tiles2, tiles2), :] * spread[j][:tiles2]
        table2[pl.ds(i * tiles2, tiles2), :] = total
        table2[pl.ds((4 + i) * tiles2, tiles2), :] = total
    x = smooth(operate2, table2, tiles2, right2, inv2, False, x)

    for part in range(tiles1 // 8):
        where_to = prolong1[pl.ds(part * 8, 8), :]
        low, high = where_to % LANES, where_to // LANES
        spread = [
            lookup([row_of(table2, j * tiles2 + h) for h in range(tiles2)], low, high)
            for j in range(4)
        ]
        for i in range(4):
            total = first1[pl.ds(i * tiles1 + part * 8, 8), :]
            for j in range(4):
                total = (
                    total
                    + weights1[pl.ds((i * 4 + j) * tiles1 + part * 8, 8), :] * spread[j]
                )
            table1[pl.ds(i * tiles1 + part * 8, 8), :] = total
            table1[pl.ds((4 + i) * tiles1 + part * 8, 8), :] = total
    x = smooth(operate1, table1, tiles1, right1, inv1, False, x)
    solution_ref[...] = table1[pl.ds(0, 4 * tiles1), :]
    residual_ref[...] = right1[...] - operate1(x)

    for copy in sends:
        copy.wait_send()


def per_device(streams, spans, *arrays):
    right_side = arrays[0]
    rows1, rows2, rows3 = right_side.shape[1], arrays[9].shape[1], arrays[12].shape[1]
    tiles1, tiles2 = rows1 // LANES, rows2 // LANES
    exchanges = 4 * KSM + 1
    f32, i32 = jnp.float32, jnp.int32
    vmem = pltpu.VMEM
    scratch = [vmem(v.shape, v.dtype) for v in arrays]
    scratch += [
        vmem((4 * tiles1, LANES), f32),
        vmem((128 * tiles1, LANES), f32),
        vmem((8 * tiles1, LANES), i32),
        vmem((8, LANES), i32),
        vmem((16, LANES), i32),
        vmem((tiles1, LANES), i32),
        vmem((16 * tiles1, LANES), f32),
        vmem((4 * tiles1, LANES), f32),
        vmem((128 * tiles2, LANES), f32),
        vmem((8 * tiles2, LANES), i32),
        vmem((8, LANES), i32),
        vmem((8, LANES), i32),
        vmem((8, LANES), i32),
        vmem((16 * tiles2, LANES), f32),
        vmem((4 * tiles2, LANES), f32),
        vmem((tiles1, LANES), i32),
        vmem((8 * tiles1, LANES), f32),
        vmem((8 * tiles2, LANES), f32),
        vmem((4 * tiles1, LANES), f32),
        vmem((4 * tiles2, LANES), f32),
        vmem((4 * tiles2, LANES), f32),
        vmem((4 * tiles1, LANES), f32),
        vmem((4 * tiles2, LANES), f32),
        vmem((4 * tiles1, LANES), f32),
        vmem((4 * tiles2, LANES), f32),
        vmem((exchanges, 8, LANES), f32),
        vmem((exchanges, 4, 8, LANES), f32),
        vmem((8, LANES), f32),
        vmem((4, 8 * tiles1, LANES), f32),
        vmem((KC - 1, 4, LANES), f32),
        vmem((KC - 1, spans, 4, LANES), f32),
        vmem((4, LANES), f32),
        vmem((4, LANES), f32),
        pltpu.SemaphoreType.DMA((len(arrays),)),
        pltpu.SemaphoreType.DMA((exchanges, 4)),
        pltpu.SemaphoreType.DMA((exchanges, 4)),
        pltpu.SemaphoreType.DMA((KC - 1, spans)),
        pltpu.SemaphoreType.DMA((KC - 1, spans)),
    ]
    out = jax.ShapeDtypeStruct((4 * tiles1, LANES), f32)
    results = pl.pallas_call(
        functools.partial(cycle_kernel, tiles1, tiles2, streams, spans),
        out_shape=(out, out),
        in_specs=[pl.BlockSpec(memory_space=pl.ANY)] * len(arrays),
        out_specs=[pl.BlockSpec(memory_space=pltpu.VMEM)] * 2,
        scratch_shapes=scratch,
        compiler_params=pltpu.CompilerParams(
            collective_id=0, has_side_effects=True, vmem_limit_bytes=48 * 1024 * 1024
        ),
        name="cycle",
    )(*arrays)
    return tuple(r.reshape(4, rows1) for r in results)


def solution(mesh):
    both = ("stream", "span")
    in_specs = (
        P(None, both),
        P(None, None, None, both),
        P(None, both),
        P(None, both),
        P(both, None),
        P(None, None, both),
        P(None, None, None, both),
        P(None, both),
        P(None, both),
        P(both, None),
        P(None, None, both),
        P(None, None, None, both),
        P(None, both),
    )
    out_specs = (P(None, both), P(None, both))
    return jax.shard_map(
        functools.partial(per_device, mesh.shape["stream"], mesh.shape["span"]),
        mesh=mesh,
        in_specs=in_specs,
        out_specs=out_specs,
        check_vma=False,
    )
```

```python
import functools

import jax
import jax.numpy as jnp
from jax import lax
from jax.experimental import pallas as pl
from jax.experimental.pallas import tpu as pltpu
from jax.sharding import PartitionSpec as P

KSM = 3
KC = 4
CHEB_CENTRE = 1.0
CHEB_RADIUS = 0.9
LANES = 128
HALF = 64
MESH = pl.DeviceIdType.MESH


def chebyshev_factors(degree):
    sigma_value = CHEB_CENTRE / CHEB_RADIUS
    rho_prev = 1.0 / sigma_value
    factors = []
    for _ in range(degree - 1):
        rho_next = 1.0 / (2.0 * sigma_value - rho_prev)
        factors.append((rho_next * rho_prev, 2.0 * rho_next / CHEB_RADIUS))
        rho_prev = rho_next
    return factors


def gather_lanes(table, places):
    return jnp.take_along_axis(table, places, axis=1, mode="promise_in_bounds")


def row_of(ref, row):
    return jnp.broadcast_to(ref[pl.ds(row, 1), :], (8, LANES))


def lookup(tables, low, high, base=0, start=None):
    picked = start
    for h, table in enumerate(tables):
        taken = gather_lanes(table, low)
        picked = taken if picked is None else jnp.where(high == h + base, taken, picked)
    return picked


def cycle_kernel(
    tiles1, tiles2, streams, spans,
    right_hbm, values1_hbm, columns1_hbm, sends1_hbm, order1_hbm, weights1_hbm,
    values2_hbm, columns2_hbm, sends2_hbm, order2_hbm, weights2_hbm,
    values3_hbm, columns3_hbm,
    solution_ref, residual_ref,
    right_in, values1_in, columns1_in, sends1_in, order1_in, weights1_in,
    values2_in, columns2_in, sends2_in, order2_in, weights2_in,
    values3_in, columns3_in,
    right1, values1, columns1, picks1, restrict1, prolong1, weights1, inv1,
    values2, columns2, picks2, restrict2, prolong2, weights2, inv2,
    order_rows, table1, table2, first1, first2, right2, part1, part2, product1, product2,
    outgoing, incoming, halo, gathered, group_own, group_all, table3, inv3,
    in_sem, send_sem, recv_sem, group_send_sem, group_recv_sem,
):
    a = lax.axis_index("stream")
    b = lax.axis_index("span")
    prev_a, next_a = lax.rem(a + streams - 1, streams), lax.rem(a + 1, streams)
    prev_b, next_b = lax.rem(b + spans - 1, spans), lax.rem(b + 1, spans)

    barrier = pltpu.get_barrier_semaphore()
    for who in (prev_a, next_a):
        pl.semaphore_signal(barrier, inc=1, device_id=(who, b), device_id_type=MESH)
    for step in range(1, spans):
        pl.semaphore_signal(
            barrier, inc=1, device_id=(a, lax.rem(b + step, spans)), device_id_type=MESH
        )

    loads = [
        pltpu.make_async_copy(src, dst, in_sem.at[n])
        for n, (src, dst) in enumerate(
            (
                (right_hbm, right_in), (values1_hbm, values1_in), (columns1_hbm, columns1_in),
                (sends1_hbm, sends1_in), (order1_hbm, order1_in), (weights1_hbm, weights1_in),
                (values2_hbm, values2_in), (columns2_hbm, columns2_in), (sends2_hbm, sends2_in),
                (order2_hbm, order2_in), (weights2_hbm, weights2_in),
                (values3_hbm, values3_in), (columns3_hbm, columns3_in),
            )
        )
    ]
    for load in loads:
        load.start()
    for load in loads:
        load.wait()

    lane = lax.broadcasted_iota(jnp.int32, (8, LANES), 1)
    row = lax.broadcasted_iota(jnp.int32, (8, LANES), 0)

    def dense_blocks(source, target, tiles):
        for k in range(8):
            for i in range(4):
                for t in range(tiles):
                    target[pl.ds((k * 16 + i * 4) * tiles + t, 4, stride=tiles), :] = source[
                        k, i, :, t * LANES : (t + 1) * LANES
                    ]

    def dense_weights(source, target, tiles):
        for i in range(4):
            for t in range(tiles):
                target[pl.ds(i * 4 * tiles + t, 4, stride=tiles), :] = source[
                    i, :, t * LANES : (t + 1) * LANES
                ]

    dense_blocks(values1_in, values1, tiles1)
    for t in range(tiles1):
        right1[pl.ds(t, 4, stride=tiles1), :] = right_in[:, t * LANES : (t + 1) * LANES]
        columns1[pl.ds(t, 8, stride=tiles1), :] = columns1_in[:, t * LANES : (t + 1) * LANES]
    for i in range(4):
        inv1[pl.ds(i * tiles1, tiles1), :] = 1.0 / values1[pl.ds(i * 5 * tiles1, tiles1), :]

    def pick_places(sends):
        stream_part = jnp.concatenate([sends[1:2, :], sends[0:1, :]], axis=1)
        span_part = jnp.concatenate([sends[3:4, :], sends[2:3, :]], axis=1)
        return jnp.where(
            row < 4,
            jnp.broadcast_to(stream_part, (8, LANES)),
            jnp.broadcast_to(span_part, (8, LANES)),
        )

    picks1[...] = pick_places(sends1_in)
    picks2[...] = pick_places(sends2_in)

    for i in range(4):
        for k in range(8):
            for t in range(tiles2):
                values2[pl.ds(i * 32 * tiles2 + k * tiles2 + t, 4, stride=8 * tiles2), :] = (
                    values2_in[k, i, :, t * LANES : (t + 1) * LANES]
                )
    for t in range(tiles2):
        columns2[pl.ds(t, 8, stride=tiles2), :] = columns2_in[:, t * LANES : (t + 1) * LANES]
    for i in range(4):
        inv2[pl.ds(i * tiles2, tiles2), :] = 1.0 / values2[pl.ds(i * 5 * 8 * tiles2, tiles2), :]
    dense_weights(weights1_in, weights1, tiles1)
    dense_weights(weights2_in, weights2, tiles2)

    quad = lane // 32
    for t in range(tiles1):
        order_rows[pl.ds(t, 1), :] = order1_in[:, t * LANES : (t + 1) * LANES]
    for pair in range(2):
        entry = row // 4 + 2 * pair
        low = (lane * 4 + entry) % LANES
        found = None
        for q in range(4):
            rows = order_rows[pl.ds(q, 4, stride=4), :]
            taken = gather_lanes(jnp.concatenate([rows, rows], axis=0), low)
            found = taken if found is None else jnp.where(quad == q, taken, found)
        restrict1[pl.ds(pair * 8, 8), :] = found

    def inverse_order(rows_ref, count, tiles):
        total = jnp.zeros((2 * tiles, LANES), jnp.float32)
        for t in range(count):
            own = rows_ref[pl.ds(t, 1), :]
            tile_ids = lax.broadcasted_iota(jnp.int32, (tiles, LANES), 0)
            member = (jnp.broadcast_to(own // LANES, (tiles, LANES)) == tile_ids)
            lanes = lax.broadcasted_iota(jnp.int32, (tiles, LANES), 1)
            small = jnp.where(member, (lanes // 4).astype(jnp.float32), 0.0)
            large = jnp.where(member, float(t), 0.0)
            left = jnp.concatenate([small, large], axis=0)
            low_ids = lax.broadcasted_iota(jnp.int32, (LANES, LANES), 0)
            right = jnp.where(
                jnp.broadcast_to(own % LANES, (LANES, LANES)) == low_ids, 1.0, 0.0
            )
            total = total + lax.dot_general(
                left.astype(jnp.bfloat16),
                right.astype(jnp.bfloat16),
                (((1,), (1,)), ((), ())),
                preferred_element_type=jnp.float32,
            )
        return (total[:tiles] + 32.0 * total[tiles:]).astype(jnp.int32)

    prolong1[...] = inverse_order(order_rows, tiles1, tiles1)

    for t in range(tiles2):
        order_rows[pl.ds(t, 1), :] = order2_in[:, t * LANES : (t + 1) * LANES]
    low = (lane * 4 + row % 4) % LANES
    found = None
    for q in range(4):
        taken = gather_lanes(row_of(order_rows, q), low)
        found = taken if found is None else jnp.where(quad == q, taken, found)
    restrict2[...] = found
    prolong2[...] = inverse_order(order_rows, tiles2, 8)

    @pl.when(b == 0)
    def _():
        incoming[:, 2] = jnp.zeros((incoming.shape[0], 8, LANES), jnp.float32)

    @pl.when(b == spans - 1)
    def _():
        incoming[:, 3] = jnp.zeros((incoming.shape[0], 8, LANES), jnp.float32)

    pl.semaphore_wait(barrier, spans + 1)

    sends = []

    def copies_of(x):
        places = (
            (1, (prev_a, b), None, None),
            (0, (next_a, b), None, None),
            (3, (a, prev_b), b > 0, b < spans - 1),
            (2, (a, next_b), b < spans - 1, b > 0),
        )
        return [
            (
                pltpu.make_async_remote_copy(
                    src_ref=outgoing.at[x],
                    dst_ref=incoming.at[x, slot],
                    send_sem=send_sem.at[x, slot],
                    recv_sem=recv_sem.at[x, slot],
                    device_id=who,
                    device_id_type=MESH,
                ),
                sends_it,
                gets_it,
            )
            for slot, who, sends_it, gets_it in places
        ]

    def when(condition, action):
        if condition is None:
            action()
        else:
            pl.when(condition)(action)

    def exchange_start(x, table, picks, tiles):
        places = picks[...]
        tables = [table[pl.ds(h, 8, stride=tiles), :] for h in range(tiles)]
        outgoing[x] = lookup(tables, places % LANES, places // LANES)
        for copy, sends_it, _ in copies_of(x):
            when(sends_it, copy.start)
            sends.append((sends_it, copy))

    def exchange_end(x):
        for copy, _, gets_it in copies_of(x):
            when(gets_it, copy.wait_recv)
        first_half = lane < HALF
        halo[...] = jnp.where(
            row < 4,
            jnp.where(first_half, incoming[x, 0], incoming[x, 1]),
            jnp.where(first_half, incoming[x, 2], incoming[x, 3]),
        )

    def store_table(table, vector, tiles):
        table[pl.ds(0, 4 * tiles), :] = vector
        table[pl.ds(4 * tiles, 4 * tiles), :] = vector

    def operate1(x):
        exchange_start(x, table1, picks1, tiles1)

        def local(group, carry):
            where_to = columns1[pl.ds(pl.multiple_of(group * 8, 8), 8), :]
            low, high = where_to % LANES, where_to // LANES
            for j in range(4):
                gathered[j, pl.ds(pl.multiple_of(group * 8, 8), 8), :] = lookup(
                    [row_of(table1, j * tiles1 + h) for h in range(tiles1)], low, high
                )
            return carry

        lax.fori_loop(0, tiles1, local, 0)
        exchange_end(x)

        def remote(part, carry):
            sums = [None] * 4
            for k in range(8):
                start = k * tiles1 + part * 8
                here = pl.ds(pl.multiple_of(start, 8), 8)
                where_to = columns1[here, :]
                low, high = where_to % LANES, where_to // LANES
                for j in range(4):
                    found = lookup(
                        [row_of(halo, j), row_of(halo, 4 + j)],
                        low, high, tiles1, gathered[j, here, :],
                    )
                    for i in range(4):
                        at = (k * 16 + i * 4 + j) * tiles1 + part * 8
                        term = values1[pl.ds(pl.multiple_of(at, 8), 8), :] * found
                        sums[i] = term if sums[i] is None else sums[i] + term
            for i in range(4):
                part1[pl.ds(pl.multiple_of(i * tiles1 + part * 8, 8), 8), :] = sums[i]
            return carry

        lax.fori_loop(0, tiles1 // 8, remote, 0)
        return part1[...]

    def operate2(x):
        exchange_start(x, table2, picks2, tiles2)
        groups = 8 * tiles2 // 8

        def local(group, carry):
            where_to = columns2[pl.ds(pl.multiple_of(group * 8, 8), 8), :]
            low, high = where_to % LANES, where_to // LANES
            for j in range(4):
                gathered[j, pl.ds(pl.multiple_of(group * 8, 8), 8), :] = lookup(
                    [row_of(table2, j * tiles2 + h) for h in range(tiles2)], low, high
                )
            return carry

        lax.fori_loop(0, groups, local, 0)
        exchange_end(x)
        sums = [None] * 4
        for group in range(groups):
            here = pl.ds(group * 8, 8)
            where_to = columns2[here, :]
            low, high = where_to % LANES, where_to // LANES
            for j in range(4):
                found = lookup(
                    [row_of(halo, j), row_of(halo, 4 + j)],
                    low, high, tiles2, gathered[j, here, :],
                )
                for i in range(4):
                    term = values2[pl.ds((i * 4 + j) * 8 * tiles2 + group * 8, 8), :] * found
                    sums[i] = term if sums[i] is None else sums[i] + term
        for i in range(4):
            part2[pl.ds(i * tiles2, tiles2), :] = sums[i][:4] + sums[i][4:]
        return part2[...]

    def smooth(operate, table, tiles, right, inv, first, x):
        if first:
            update = inv[...] * right[...]
            store_table(table, update, tiles)
        else:
            update = inv[...] * (right[...] - operate(x))
            x += 1
            store_table(table, table[pl.ds(0, 4 * tiles), :] + update, tiles)
        for keep, gain in chebyshev_factors(KSM):
            current = right[...] - operate(x)
            x += 1
            update = keep * update + gain * (inv[...] * current)
            store_table(table, table[pl.ds(0, 4 * tiles), :] + update, tiles)
        return x

    x = smooth(operate1, table1, tiles1, right1, inv1, True, 0)
    first1[...] = table1[pl.ds(0, 4 * tiles1), :]
    resid = right1[...] - operate1(x)
    x += 1
    part1[...] = resid
    for j in range(4):
        total = None
        for i in range(4):
            term = (
                weights1[pl.ds((i * 4 + j) * tiles1, tiles1), :]
                * part1[pl.ds(i * tiles1, tiles1), :]
            )
            total = term if total is None else total + term
        product1[pl.ds(j * tiles1, tiles1), :] = total
    for j in range(4):
        tables = [row_of(product1, j * tiles1 + h) for h in range(tiles1)]
        total = None
        for pair in range(2):
            where_to = restrict1[pl.ds(pair * 8, 8), :]
            taken = lookup(tables, where_to % LANES, where_to // LANES)
            total = taken if total is None else total + taken
        right2[pl.ds(j * tiles2, tiles2), :] = total[:4] + total[4:]

    x = smooth(operate2, table2, tiles2, right2, inv2, True, x)
    first2[...] = table2[pl.ds(0, 4 * tiles2), :]
    resid = right2[...] - operate2(x)
    x += 1
    part2[...] = resid
    for j in range(4):
        total = None
        for i in range(4):
            term = (
                weights2[pl.ds((i * 4 + j) * tiles2, tiles2), :]
                * part2[pl.ds(i * tiles2, tiles2), :]
            )
            total = term if total is None else total + term
        product2[pl.ds(j * tiles2, tiles2), :] = total
    where_to = restrict2[...]
    for j in range(4):
        tables = [row_of(product2, j * tiles2 + h) for h in range(tiles2)]
        taken = lookup(tables, where_to % LANES, where_to // LANES)
        table3[pl.ds(j, 1), :] = jnp.sum(taken[:4], axis=0, keepdims=True)

    right3 = table3[...]
    for i in range(4):
        inv3[pl.ds(i, 1), :] = 1.0 / values3_in[0, i, i : i + 1, :]
    update = inv3[...] * right3
    vector = update
    columns3 = columns3_in[...]
    low3, high3 = columns3 % LANES, columns3 // LANES
    for turn, (keep, gain) in enumerate(chebyshev_factors(KC)):
        group_own[turn] = vector
        copies = []
        for step in range(1, spans):
            copies.append(
                pltpu.make_async_remote_copy(
                    src_ref=group_own.at[turn],
                    dst_ref=group_all.at[turn, step],
                    send_sem=group_send_sem.at[turn, step],
                    recv_sem=group_recv_sem.at[turn, step],
                    device_id=(a, lax.rem(b + step, spans)),
                    device_id_type=MESH,
                )
            )
        for copy in copies:
            copy.start()
            sends.append((None, copy))
        for copy in copies:
            copy.wait_recv()
        distance = lax.rem(b - high3 + spans, spans)
        picked = []
        for j in range(4):
            tables = [row_of(group_own.at[turn], j)] + [
                row_of(group_all.at[turn, step], j) for step in range(1, spans)
            ]
            picked.append(lookup(tables, low3, distance))
        for i in range(4):
            total = None
            for j in range(4):
                term = values3_in[:, i, j, :] * picked[j]
                total = term if total is None else total + term
            table3[pl.ds(i, 1), :] = jnp.sum(total, axis=0, keepdims=True)
        current = right3 - table3[...]
        update = keep * update + gain * (inv3[...] * current)
        vector = vector + update

    table3[...] = vector
    back = prolong2[...]
    spread = [gather_lanes(row_of(table3, j), back) for j in range(4)]
    for i in range(4):
        total = first2[pl.ds(i * tiles2, tiles2), :]
        for j in range(4):
            total = total + weights2[pl.ds((i * 4 + j) * tiles2, tiles2), :] * spread[j][:tiles2]
        table2[pl.ds(i * tiles2, tiles2), :] = total
        table2[pl.ds((4 + i) * tiles2, tiles2), :] = total
    x = smooth(operate2, table2, tiles2, right2, inv2, False, x)

    for part in range(tiles1 // 8):
        where_to = prolong1[pl.ds(part * 8, 8), :]
        low, high = where_to % LANES, where_to // LANES
        spread = [
            lookup([row_of(table2, j * tiles2 + h) for h in range(tiles2)], low, high)
            for j in range(4)
        ]
        for i in range(4):
            total = first1[pl.ds(i * tiles1 + part * 8, 8), :]
            for j in range(4):
                total = (
                    total
                    + weights1[pl.ds((i * 4 + j) * tiles1 + part * 8, 8), :] * spread[j]
                )
            table1[pl.ds(i * tiles1 + part * 8, 8), :] = total
            table1[pl.ds((4 + i) * tiles1 + part * 8, 8), :] = total
    x = smooth(operate1, table1, tiles1, right1, inv1, False, x)
    solution_ref[...] = table1[pl.ds(0, 4 * tiles1), :]
    residual_ref[...] = right1[...] - operate1(x)

    for sends_it, copy in sends:
        when(sends_it, copy.wait_send)


def per_device(streams, spans, *arrays):
    right_side = arrays[0]
    rows1, rows2, rows3 = right_side.shape[1], arrays[9].shape[1], arrays[12].shape[1]
    tiles1, tiles2 = rows1 // LANES, rows2 // LANES
    exchanges = 4 * KSM + 1
    f32, i32 = jnp.float32, jnp.int32
    vmem = pltpu.VMEM
    scratch = [vmem(v.shape, v.dtype) for v in arrays]
    scratch += [
        vmem((4 * tiles1, LANES), f32),
        vmem((128 * tiles1, LANES), f32),
        vmem((8 * tiles1, LANES), i32),
        vmem((8, LANES), i32),
        vmem((16, LANES), i32),
        vmem((tiles1, LANES), i32),
        vmem((16 * tiles1, LANES), f32),
        vmem((4 * tiles1, LANES), f32),
        vmem((128 * tiles2, LANES), f32),
        vmem((8 * tiles2, LANES), i32),
        vmem((8, LANES), i32),
        vmem((8, LANES), i32),
        vmem((8, LANES), i32),
        vmem((16 * tiles2, LANES), f32),
        vmem((4 * tiles2, LANES), f32),
        vmem((tiles1, LANES), i32),
        vmem((8 * tiles1, LANES), f32),
        vmem((8 * tiles2, LANES), f32),
        vmem((4 * tiles1, LANES), f32),
        vmem((4 * tiles2, LANES), f32),
        vmem((4 * tiles2, LANES), f32),
        vmem((4 * tiles1, LANES), f32),
        vmem((4 * tiles2, LANES), f32),
        vmem((4 * tiles1, LANES), f32),
        vmem((4 * tiles2, LANES), f32),
        vmem((exchanges, 8, LANES), f32),
        vmem((exchanges, 4, 8, LANES), f32),
        vmem((8, LANES), f32),
        vmem((4, 8 * tiles1, LANES), f32),
        vmem((KC - 1, 4, LANES), f32),
        vmem((KC - 1, spans, 4, LANES), f32),
        vmem((4, LANES), f32),
        vmem((4, LANES), f32),
        pltpu.SemaphoreType.DMA((len(arrays),)),
        pltpu.SemaphoreType.DMA((exchanges, 4)),
        pltpu.SemaphoreType.DMA((exchanges, 4)),
        pltpu.SemaphoreType.DMA((KC - 1, spans)),
        pltpu.SemaphoreType.DMA((KC - 1, spans)),
    ]
    out = jax.ShapeDtypeStruct((4 * tiles1, LANES), f32)
    results = pl.pallas_call(
        functools.partial(cycle_kernel, tiles1, tiles2, streams, spans),
        out_shape=(out, out),
        in_specs=[pl.BlockSpec(memory_space=pltpu.HBM)] * len(arrays),
        out_specs=[pl.BlockSpec(memory_space=pltpu.VMEM)] * 2,
        scratch_shapes=scratch,
        compiler_params=pltpu.CompilerParams(
            collective_id=0, has_side_effects=True, vmem_limit_bytes=67_000_000
        ),
        name="cycle",
    )(*arrays)
    return tuple(r.reshape(4, rows1) for r in results)


def solution(mesh):
    both = ("stream", "span")
    in_specs = (
        P(None, both),
        P(None, None, None, both),
        P(None, both),
        P(None, both),
        P(both, None),
        P(None, None, both),
        P(None, None, None, both),
        P(None, both),
        P(None, both),
        P(both, None),
        P(None, None, both),
        P(None, None, None, both),
        P(None, both),
    )
    out_specs = (P(None, both), P(None, both))
    return jax.shard_map(
        functools.partial(per_device, mesh.shape["stream"], mesh.shape["span"]),
        mesh=mesh,
        in_specs=in_specs,
        out_specs=out_specs,
        check_vma=False,
    )
```

```python
import functools

import jax
import jax.numpy as jnp
from jax import lax
from jax.experimental import pallas as pl
from jax.experimental.pallas import tpu as pltpu
from jax.sharding import PartitionSpec as P

KSM = 3
KC = 4
CHEB_CENTRE = 1.0
CHEB_RADIUS = 0.9
LANES = 128
HALF = 64
MESH = pl.DeviceIdType.MESH


def chebyshev_factors(degree):
    sigma_value = CHEB_CENTRE / CHEB_RADIUS
    rho_prev = 1.0 / sigma_value
    factors = []
    for _ in range(degree - 1):
        rho_next = 1.0 / (2.0 * sigma_value - rho_prev)
        factors.append((rho_next * rho_prev, 2.0 * rho_next / CHEB_RADIUS))
        rho_prev = rho_next
    return factors


def sorted_far(copies):
    middle = len(copies) // 2
    return [copies[n] for n in sorted(range(len(copies)), key=lambda n: abs(n - middle))]


def gather_lanes(table, places):
    return jnp.take_along_axis(table, places, axis=1, mode="promise_in_bounds")


def row_of(ref, row):
    return jnp.broadcast_to(ref[pl.ds(row, 1), :], (8, LANES))


def lookup(tables, low, high, base=0, start=None):
    picked = start
    for h, table in enumerate(tables):
        taken = gather_lanes(table, low)
        picked = taken if picked is None else jnp.where(high == h + base, taken, picked)
    return picked


def cycle_kernel(
    tiles1, tiles2, streams, spans,
    right_hbm, values1_hbm, columns1_hbm, sends1_hbm, order1_hbm, weights1_hbm,
    values2_hbm, columns2_hbm, sends2_hbm, order2_hbm, weights2_hbm,
    values3_hbm, columns3_hbm,
    solution_ref, residual_ref,
    right_in, values1_in, columns1_in, sends1_in, order1_in, weights1_in,
    values2_in, columns2_in, sends2_in, order2_in, weights2_in,
    values3_in, columns3_in,
    right1, values1, columns1, picks1, restrict1, prolong1, weights1, inv1,
    values2, columns2, picks2, restrict2, prolong2, weights2, inv2,
    order_rows, table1, table2, first1, first2, right2, part1, part2, product1, product2,
    outgoing, incoming, halo, gathered, group_own, group_all, table3, inv3,
    in_sem, send_sem, recv_sem, group_send_sem, group_recv_sem, greet_sem,
):
    a = lax.axis_index("stream")
    b = lax.axis_index("span")
    prev_a, next_a = lax.rem(a + streams - 1, streams), lax.rem(a + 1, streams)
    prev_b, next_b = lax.rem(b + spans - 1, spans), lax.rem(b + 1, spans)

    barrier = pltpu.get_barrier_semaphore()
    for who in ((prev_a, b), (next_a, b), (a, prev_b), (a, next_b)):
        pl.semaphore_signal(barrier, inc=1, device_id=who, device_id_type=MESH)

    loads = [
        pltpu.make_async_copy(src, dst, in_sem.at[n])
        for n, (src, dst) in enumerate(
            (
                (right_hbm, right_in), (values1_hbm, values1_in), (columns1_hbm, columns1_in),
                (sends1_hbm, sends1_in), (order1_hbm, order1_in), (weights1_hbm, weights1_in),
                (values2_hbm, values2_in), (columns2_hbm, columns2_in), (sends2_hbm, sends2_in),
                (order2_hbm, order2_in), (weights2_hbm, weights2_in),
                (values3_hbm, values3_in), (columns3_hbm, columns3_in),
            )
        )
    ]
    for load in loads:
        load.start()
    for n in (0, 1, 3):
        loads[n].wait()

    lane = lax.broadcasted_iota(jnp.int32, (8, LANES), 1)
    row = lax.broadcasted_iota(jnp.int32, (8, LANES), 0)

    def dense_blocks(source, target, tiles):
        for k in range(8):
            for i in range(4):
                for t in range(tiles):
                    target[pl.ds((k * 16 + i * 4) * tiles + t, 4, stride=tiles), :] = source[
                        k, i, :, t * LANES : (t + 1) * LANES
                    ]

    def dense_weights(source, target, tiles):
        for i in range(4):
            for t in range(tiles):
                target[pl.ds(i * 4 * tiles + t, 4, stride=tiles), :] = source[
                    i, :, t * LANES : (t + 1) * LANES
                ]

    for t in range(tiles1):
        right1[pl.ds(t, 4, stride=tiles1), :] = right_in[:, t * LANES : (t + 1) * LANES]
        for i in range(4):
            inv1[pl.ds(i * tiles1 + t, 1), :] = values1_in[
                0, i, i : i + 1, t * LANES : (t + 1) * LANES
            ]
    inv1[...] = 1.0 / inv1[...]

    def arrange_fine():
        loads[2].wait()
        dense_blocks(values1_in, values1, tiles1)
        for t in range(tiles1):
            columns1[pl.ds(t, 8, stride=tiles1), :] = columns1_in[:, t * LANES : (t + 1) * LANES]

    def pick_places(sends):
        stream_part = jnp.concatenate([sends[1:2, :], sends[0:1, :]], axis=1)
        span_part = jnp.concatenate([sends[3:4, :], sends[2:3, :]], axis=1)
        return jnp.where(
            row < 4,
            jnp.broadcast_to(stream_part, (8, LANES)),
            jnp.broadcast_to(span_part, (8, LANES)),
        )

    picks1[...] = pick_places(sends1_in)

    def inverse_order(rows_ref, count, tiles):
        total = jnp.zeros((2 * tiles, LANES), jnp.float32)
        for t in range(count):
            own = rows_ref[pl.ds(t, 1), :]
            tile_ids = lax.broadcasted_iota(jnp.int32, (tiles, LANES), 0)
            member = (jnp.broadcast_to(own // LANES, (tiles, LANES)) == tile_ids)
            lanes = lax.broadcasted_iota(jnp.int32, (tiles, LANES), 1)
            small = jnp.where(member, (lanes // 4).astype(jnp.float32), 0.0)
            large = jnp.where(member, float(t), 0.0)
            left = jnp.concatenate([small, large], axis=0)
            low_ids = lax.broadcasted_iota(jnp.int32, (LANES, LANES), 0)
            right = jnp.where(
                jnp.broadcast_to(own % LANES, (LANES, LANES)) == low_ids, 1.0, 0.0
            )
            total = total + lax.dot_general(
                left.astype(jnp.bfloat16),
                right.astype(jnp.bfloat16),
                (((1,), (1,)), ((), ())),
                preferred_element_type=jnp.float32,
            )
        return (total[:tiles] + 32.0 * total[tiles:]).astype(jnp.int32)

    def arrange_middle():
        for n in (5, 6, 7, 8, 10):
            loads[n].wait()
        picks2[...] = pick_places(sends2_in)
        for i in range(4):
            for k in range(8):
                for t in range(tiles2):
                    values2[pl.ds(i * 32 * tiles2 + k * tiles2 + t, 4, stride=8 * tiles2), :] = (
                        values2_in[k, i, :, t * LANES : (t + 1) * LANES]
                    )
        for t in range(tiles2):
            columns2[pl.ds(t, 8, stride=tiles2), :] = columns2_in[:, t * LANES : (t + 1) * LANES]
        for i in range(4):
            inv2[pl.ds(i * tiles2, tiles2), :] = 1.0 / values2[pl.ds(i * 5 * 8 * tiles2, tiles2), :]
        dense_weights(weights1_in, weights1, tiles1)
        dense_weights(weights2_in, weights2, tiles2)

    def arrange_orders():
        for n in (4, 9, 11, 12):
            loads[n].wait()
        quad = lane // 32
        for t in range(tiles1):
            order_rows[pl.ds(t, 1), :] = order1_in[:, t * LANES : (t + 1) * LANES]
        for pair in range(2):
            entry = row // 4 + 2 * pair
            low = (lane * 4 + entry) % LANES
            found = None
            for q in range(4):
                rows = order_rows[pl.ds(q, 4, stride=4), :]
                taken = gather_lanes(jnp.concatenate([rows, rows], axis=0), low)
                found = taken if found is None else jnp.where(quad == q, taken, found)
            restrict1[pl.ds(pair * 8, 8), :] = found

        prolong1[...] = inverse_order(order_rows, tiles1, tiles1)

        for t in range(tiles2):
            order_rows[pl.ds(t, 1), :] = order2_in[:, t * LANES : (t + 1) * LANES]
        low = (lane * 4 + row % 4) % LANES
        found = None
        for q in range(4):
            taken = gather_lanes(row_of(order_rows, q), low)
            found = taken if found is None else jnp.where(quad == q, taken, found)
        restrict2[...] = found
        prolong2[...] = inverse_order(order_rows, tiles2, 8)

    background = {0: arrange_fine, 1: arrange_middle, 2: arrange_orders}

    @pl.when(b == 0)
    def _():
        incoming[:, 2] = jnp.zeros((incoming.shape[0], 8, LANES), jnp.float32)

    @pl.when(b == spans - 1)
    def _():
        incoming[:, 3] = jnp.zeros((incoming.shape[0], 8, LANES), jnp.float32)

    pl.semaphore_wait(barrier, 4)

    def greet(stage):
        for step in (1 << stage, spans - (1 << stage)):
            pl.semaphore_signal(
                greet_sem.at[stage],
                inc=1,
                device_id=(a, lax.rem(b + step, spans)),
                device_id_type=MESH,
            )

    stages = max((spans // 2 - 1).bit_length(), 0)
    sends = []

    def copies_of(x):
        places = (
            (1, (prev_a, b), None, None),
            (0, (next_a, b), None, None),
            (3, (a, prev_b), b > 0, b < spans - 1),
            (2, (a, next_b), b < spans - 1, b > 0),
        )
        return [
            (
                pltpu.make_async_remote_copy(
                    src_ref=outgoing.at[x],
                    dst_ref=incoming.at[x, slot],
                    send_sem=send_sem.at[x, slot],
                    recv_sem=recv_sem.at[x, slot],
                    device_id=who,
                    device_id_type=MESH,
                ),
                sends_it,
                gets_it,
            )
            for slot, who, sends_it, gets_it in places
        ]

    def when(condition, action):
        if condition is None:
            action()
        else:
            pl.when(condition)(action)

    def exchange_start(x, table, picks, tiles):
        places = picks[...]
        tables = [table[pl.ds(h, 8, stride=tiles), :] for h in range(tiles)]
        outgoing[x] = lookup(tables, places % LANES, places // LANES)
        for copy, sends_it, _ in copies_of(x):
            when(sends_it, copy.start)
            sends.append((sends_it, copy))
        if x < stages:
            greet(x)

    def exchange_end(x):
        for copy, _, gets_it in copies_of(x):
            when(gets_it, copy.wait_recv)
        if x < stages:
            pl.semaphore_wait(greet_sem.at[x], 2)
        first_half = lane < HALF
        halo[...] = jnp.where(
            row < 4,
            jnp.where(first_half, incoming[x, 0], incoming[x, 1]),
            jnp.where(first_half, incoming[x, 2], incoming[x, 3]),
        )

    def store_table(table, vector, tiles):
        table[pl.ds(0, 4 * tiles), :] = vector
        table[pl.ds(4 * tiles, 4 * tiles), :] = vector

    def operate1(x):
        exchange_start(x, table1, picks1, tiles1)
        if x in background:
            background[x]()

        def local(group, carry):
            where_to = columns1[pl.ds(pl.multiple_of(group * 8, 8), 8), :]
            low, high = where_to % LANES, where_to // LANES
            for j in range(4):
                gathered[j, pl.ds(pl.multiple_of(group * 8, 8), 8), :] = lookup(
                    [row_of(table1, j * tiles1 + h) for h in range(tiles1)], low, high
                )
            return carry

        lax.fori_loop(0, tiles1, local, 0)
        exchange_end(x)

        def remote(part, carry):
            sums = [None] * 4
            for k in range(8):
                start = k * tiles1 + part * 8
                here = pl.ds(pl.multiple_of(start, 8), 8)
                where_to = columns1[here, :]
                low, high = where_to % LANES, where_to // LANES
                for j in range(4):
                    found = lookup(
                        [row_of(halo, j), row_of(halo, 4 + j)],
                        low, high, tiles1, gathered[j, here, :],
                    )
                    for i in range(4):
                        at = (k * 16 + i * 4 + j) * tiles1 + part * 8
                        term = values1[pl.ds(pl.multiple_of(at, 8), 8), :] * found
                        sums[i] = term if sums[i] is None else sums[i] + term
            for i in range(4):
                part1[pl.ds(pl.multiple_of(i * tiles1 + part * 8, 8), 8), :] = sums[i]
            return carry

        lax.fori_loop(0, tiles1 // 8, remote, 0)
        return part1[...]

    def operate2(x):
        exchange_start(x, table2, picks2, tiles2)
        groups = 8 * tiles2 // 8

        def local(group, carry):
            where_to = columns2[pl.ds(pl.multiple_of(group * 8, 8), 8), :]
            low, high = where_to % LANES, where_to // LANES
            for j in range(4):
                gathered[j, pl.ds(pl.multiple_of(group * 8, 8), 8), :] = lookup(
                    [row_of(table2, j * tiles2 + h) for h in range(tiles2)], low, high
                )
            return carry

        lax.fori_loop(0, groups, local, 0)
        exchange_end(x)
        sums = [None] * 4
        for group in range(groups):
            here = pl.ds(group * 8, 8)
            where_to = columns2[here, :]
            low, high = where_to % LANES, where_to // LANES
            for j in range(4):
                found = lookup(
                    [row_of(halo, j), row_of(halo, 4 + j)],
                    low, high, tiles2, gathered[j, here, :],
                )
                for i in range(4):
                    term = values2[pl.ds((i * 4 + j) * 8 * tiles2 + group * 8, 8), :] * found
                    sums[i] = term if sums[i] is None else sums[i] + term
        for i in range(4):
            part2[pl.ds(i * tiles2, tiles2), :] = sums[i][:4] + sums[i][4:]
        return part2[...]

    def smooth(operate, table, tiles, right, inv, first, x):
        if first:
            update = inv[...] * right[...]
            store_table(table, update, tiles)
        else:
            update = inv[...] * (right[...] - operate(x))
            x += 1
            store_table(table, table[pl.ds(0, 4 * tiles), :] + update, tiles)
        for keep, gain in chebyshev_factors(KSM):
            current = right[...] - operate(x)
            x += 1
            update = keep * update + gain * (inv[...] * current)
            store_table(table, table[pl.ds(0, 4 * tiles), :] + update, tiles)
        return x

    x = smooth(operate1, table1, tiles1, right1, inv1, True, 0)
    first1[...] = table1[pl.ds(0, 4 * tiles1), :]
    resid = right1[...] - operate1(x)
    x += 1
    part1[...] = resid
    for j in range(4):
        total = None
        for i in range(4):
            term = (
                weights1[pl.ds((i * 4 + j) * tiles1, tiles1), :]
                * part1[pl.ds(i * tiles1, tiles1), :]
            )
            total = term if total is None else total + term
        product1[pl.ds(j * tiles1, tiles1), :] = total
    for j in range(4):
        tables = [row_of(product1, j * tiles1 + h) for h in range(tiles1)]
        total = None
        for pair in range(2):
            where_to = restrict1[pl.ds(pair * 8, 8), :]
            taken = lookup(tables, where_to % LANES, where_to // LANES)
            total = taken if total is None else total + taken
        right2[pl.ds(j * tiles2, tiles2), :] = total[:4] + total[4:]

    x = smooth(operate2, table2, tiles2, right2, inv2, True, x)
    first2[...] = table2[pl.ds(0, 4 * tiles2), :]
    resid = right2[...] - operate2(x)
    x += 1
    part2[...] = resid
    for j in range(4):
        total = None
        for i in range(4):
            term = (
                weights2[pl.ds((i * 4 + j) * tiles2, tiles2), :]
                * part2[pl.ds(i * tiles2, tiles2), :]
            )
            total = term if total is None else total + term
        product2[pl.ds(j * tiles2, tiles2), :] = total
    where_to = restrict2[...]
    for j in range(4):
        tables = [row_of(product2, j * tiles2 + h) for h in range(tiles2)]
        taken = lookup(tables, where_to % LANES, where_to // LANES)
        table3[pl.ds(j, 1), :] = jnp.sum(taken[:4], axis=0, keepdims=True)

    right3 = table3[...]
    for i in range(4):
        inv3[pl.ds(i, 1), :] = 1.0 / values3_in[0, i, i : i + 1, :]
    update = inv3[...] * right3
    vector = update
    columns3 = columns3_in[...]
    low3, high3 = columns3 % LANES, columns3 // LANES
    for turn, (keep, gain) in enumerate(chebyshev_factors(KC)):
        group_own[turn] = vector
        copies = []
        for step in range(1, spans):
            copies.append(
                pltpu.make_async_remote_copy(
                    src_ref=group_own.at[turn],
                    dst_ref=group_all.at[turn, step],
                    send_sem=group_send_sem.at[turn, step],
                    recv_sem=group_recv_sem.at[turn, step],
                    device_id=(a, lax.rem(b + step, spans)),
                    device_id_type=MESH,
                )
            )
        for copy in sorted_far(copies):
            copy.start()
            sends.append((None, copy))
        for copy in copies:
            copy.wait_recv()
        distance = lax.rem(b - high3 + spans, spans)
        picked = []
        for j in range(4):
            tables = [row_of(group_own.at[turn], j)] + [
                row_of(group_all.at[turn, step], j) for step in range(1, spans)
            ]
            picked.append(lookup(tables, low3, distance))
        for i in range(4):
            total = None
            for j in range(4):
                term = values3_in[:, i, j, :] * picked[j]
                total = term if total is None else total + term
            table3[pl.ds(i, 1), :] = jnp.sum(total, axis=0, keepdims=True)
        current = right3 - table3[...]
        update = keep * update + gain * (inv3[...] * current)
        vector = vector + update

    table3[...] = vector
    back = prolong2[...]
    spread = [gather_lanes(row_of(table3, j), back) for j in range(4)]
    for i in range(4):
        total = first2[pl.ds(i * tiles2, tiles2), :]
        for j in range(4):
            total = total + weights2[pl.ds((i * 4 + j) * tiles2, tiles2), :] * spread[j][:tiles2]
        table2[pl.ds(i * tiles2, tiles2), :] = total
        table2[pl.ds((4 + i) * tiles2, tiles2), :] = total
    x = smooth(operate2, table2, tiles2, right2, inv2, False, x)

    for part in range(tiles1 // 8):
        where_to = prolong1[pl.ds(part * 8, 8), :]
        low, high = where_to % LANES, where_to // LANES
        spread = [
            lookup([row_of(table2, j * tiles2 + h) for h in range(tiles2)], low, high)
            for j in range(4)
        ]
        for i in range(4):
            total = first1[pl.ds(i * tiles1 + part * 8, 8), :]
            for j in range(4):
                total = (
                    total
                    + weights1[pl.ds((i * 4 + j) * tiles1 + part * 8, 8), :] * spread[j]
                )
            table1[pl.ds(i * tiles1 + part * 8, 8), :] = total
            table1[pl.ds((4 + i) * tiles1 + part * 8, 8), :] = total
    x = smooth(operate1, table1, tiles1, right1, inv1, False, x)
    for t in range(tiles1):
        solution_ref[:, t * LANES : (t + 1) * LANES] = table1[pl.ds(t, 4, stride=tiles1), :]
    part1[...] = right1[...] - operate1(x)
    for t in range(tiles1):
        residual_ref[:, t * LANES : (t + 1) * LANES] = part1[pl.ds(t, 4, stride=tiles1), :]

    for sends_it, copy in sends:
        when(sends_it, copy.wait_send)


def per_device(streams, spans, *arrays):
    right_side = arrays[0]
    rows1, rows2, rows3 = right_side.shape[1], arrays[9].shape[1], arrays[12].shape[1]
    tiles1, tiles2 = rows1 // LANES, rows2 // LANES
    exchanges = 4 * KSM + 1
    f32, i32 = jnp.float32, jnp.int32
    vmem = pltpu.VMEM
    scratch = [vmem(v.shape, v.dtype) for v in arrays]
    scratch += [
        vmem((4 * tiles1, LANES), f32),
        vmem((128 * tiles1, LANES), f32),
        vmem((8 * tiles1, LANES), i32),
        vmem((8, LANES), i32),
        vmem((16, LANES), i32),
        vmem((tiles1, LANES), i32),
        vmem((16 * tiles1, LANES), f32),
        vmem((4 * tiles1, LANES), f32),
        vmem((128 * tiles2, LANES), f32),
        vmem((8 * tiles2, LANES), i32),
        vmem((8, LANES), i32),
        vmem((8, LANES), i32),
        vmem((8, LANES), i32),
        vmem((16 * tiles2, LANES), f32),
        vmem((4 * tiles2, LANES), f32),
        vmem((tiles1, LANES), i32),
        vmem((8 * tiles1, LANES), f32),
        vmem((8 * tiles2, LANES), f32),
        vmem((4 * tiles1, LANES), f32),
        vmem((4 * tiles2, LANES), f32),
        vmem((4 * tiles2, LANES), f32),
        vmem((4 * tiles1, LANES), f32),
        vmem((4 * tiles2, LANES), f32),
        vmem((4 * tiles1, LANES), f32),
        vmem((4 * tiles2, LANES), f32),
        vmem((exchanges, 8, LANES), f32),
        vmem((exchanges, 4, 8, LANES), f32),
        vmem((8, LANES), f32),
        vmem((4, 8 * tiles1, LANES), f32),
        vmem((KC - 1, 4, LANES), f32),
        vmem((KC - 1, spans, 4, LANES), f32),
        vmem((4, LANES), f32),
        vmem((4, LANES), f32),
        pltpu.SemaphoreType.DMA((len(arrays),)),
        pltpu.SemaphoreType.DMA((exchanges, 4)),
        pltpu.SemaphoreType.DMA((exchanges, 4)),
        pltpu.SemaphoreType.DMA((KC - 1, spans)),
        pltpu.SemaphoreType.DMA((KC - 1, spans)),
        pltpu.SemaphoreType.REGULAR((4,)),
    ]
    out = jax.ShapeDtypeStruct((4, rows1), f32)
    return pl.pallas_call(
        functools.partial(cycle_kernel, tiles1, tiles2, streams, spans),
        out_shape=(out, out),
        in_specs=[pl.BlockSpec(memory_space=pltpu.HBM)] * len(arrays),
        out_specs=[pl.BlockSpec(memory_space=pltpu.VMEM)] * 2,
        scratch_shapes=scratch,
        compiler_params=pltpu.CompilerParams(
            collective_id=0, has_side_effects=True, vmem_limit_bytes=67_000_000
        ),
        name="cycle",
    )(*arrays)


def solution(mesh):
    both = ("stream", "span")
    in_specs = (
        P(None, both),
        P(None, None, None, both),
        P(None, both),
        P(None, both),
        P(both, None),
        P(None, None, both),
        P(None, None, None, both),
        P(None, both),
        P(None, both),
        P(both, None),
        P(None, None, both),
        P(None, None, None, both),
        P(None, both),
    )
    out_specs = (P(None, both), P(None, both))
    return jax.shard_map(
        functools.partial(per_device, mesh.shape["stream"], mesh.shape["span"]),
        mesh=mesh,
        in_specs=in_specs,
        out_specs=out_specs,
        check_vma=False,
    )
```
